256 devices in a mesh: tok: 32 (over z_lo, x, core), head: 8 (over y, z_hi).
Axes of the slice: x: 4, y: 4, z: 8 (z_hi: 2, z_lo: 4; z = z_hi * 4 + z_lo), core: 2. Of those that a mesh axis runs over, the one named last changes fastest.
Arguments:
- queries: bfloat16 [2, 2, 8192, 8192], P(None, None, 'tok', 'head'), may hold values from -6 to 6
- first_keys: bfloat16 [2, 8192, 8192], P(None, 'tok', 'head'), may hold values from -6 to 6
- first_values: bfloat16 [2, 8192, 8192], P(None, 'tok', 'head'), may hold values from -6 to 6
- first_rates: float32 [2, 16, 8192], P(None, 'head', 'tok'), may hold values from 0.1 to 1
- w_one: bfloat16 [16, 512, 512], P('head'), may hold values from -0.25 to 0.25
- w_three: bfloat16 [16, 512, 512], P('head'), may hold values from -0.25 to 0.25
- w_two: bfloat16 [16, 512, 512], P('head'), may hold values from -0.25 to 0.25
- step_size: float32 [16], P('head'), may hold values from 0.02 to 0.06
- out_gain: float32 [8192], replicated, may hold values from 0.25 to 1.75
Outputs:
- normed_rows: bfloat16 [2, 2, 8192, 8192], P(None, None, ('tok', 'head'))
The draws below stay inside these ranges and needn't reach their ends.
All inputs are finite; a program needn't handle non-finite values.
Results may differ from the reference program's by a relative error of at most 0.025.
Values may be sent and summed in bfloat16 or wider, within the bound.
No kernel may reach another device: no remote copies, remote signals or barrier semaphores. Data moves between devices by JAX's collectives and lax.ppermute only.
A program may use at most 64 MiB of HBM per device.

```python
import math
import jax
import jax.numpy as jnp
from jax import lax

HEADS = 16
HD = 512
HH = 512
SEQS = 2
GROUPS = 2
CTOK = 256
GROUP = 8192
WIDTH = 8192
N_TOK = 32


def levels(own_key, extent, cuts, smallest, top_value):
    def one(dim, blocks):
        draws = jax.random.uniform(jax.random.fold_in(jax.random.fold_in(own_key, 6), dim), (blocks,), jnp.float32, smallest / len(cuts), top_value / len(cuts))
        return jnp.repeat(jnp.exp(draws), extent[dim] // blocks).reshape((-1,) + (1,) * (len(extent) - dim - 1))

    level = one(*cuts[0])
    for cut in cuts[1:]:
        level = level * one(*cut)
    return level


def bell_draw(stream_key, extent, spread, reach, shards=(), kind=jnp.bfloat16):
    level = levels(stream_key, extent, shards, -0.22, 0.18) if shards else 1.0
    drawn = jax.random.normal(stream_key, extent, jnp.float32) * spread * level
    return jnp.minimum(jnp.maximum(drawn, -reach), reach).astype(kind)


def setup_inputs(seed: int = 0) -> dict:
    splits = jax.random.split(jax.random.key(seed), 10)
    return {
        "queries": bell_draw(splits[0], (SEQS, GROUPS, GROUP, WIDTH), 1.0, 6.0, ((2, 32), (3, 8))),
        "first_keys": bell_draw(splits[1], (SEQS, GROUP, WIDTH), 1.0, 6.0, ((1, 32), (2, 8))),
        "first_values": bell_draw(splits[2], (SEQS, GROUP, WIDTH), 1.0, 6.0, ((1, 32), (2, 8))),
        "first_rates": jnp.clip(jnp.exp(math.log(1.0) - 2.3025851 * jax.random.uniform(splits[3], (SEQS, HEADS, GROUP), jnp.float32) ** levels(splits[3], (SEQS, HEADS, GROUP), ((1, 8), (2, 32)), -0.2, 0.2)), 0.1, 1.0),
        "w_one": bell_draw(splits[4], (HEADS, HD, HH), HD ** -0.5, 0.25, ((0, 8),)),
        "w_three": bell_draw(splits[5], (HEADS, HD, HH), HD ** -0.5, 0.25, ((0, 8),)),
        "w_two": bell_draw(splits[6], (HEADS, HH, HD), HH ** -0.5, 0.25, ((0, 8),)),
        "step_size": jnp.clip(jnp.exp(math.log(0.06) - 1.0986123 * jax.random.uniform(splits[7], (HEADS,), jnp.float32) ** levels(splits[7], (HEADS,), ((0, 8),), -0.2, 0.2)), 0.02, 0.06),
        "out_gain": jnp.clip(1.0 + 0.15 * jax.random.normal(splits[8], (WIDTH,), jnp.float32), 0.25, 1.75),
    }


def swiglu_apply(inputs, w_one, w_three, w_two):
    gate_pre = jnp.einsum('...a,ab->...b', inputs.astype(jnp.float32), w_one.astype(jnp.float32))
    up_pre = jnp.einsum('...a,ab->...b', inputs.astype(jnp.float32), w_three.astype(jnp.float32))
    hidden = (gate_pre * jax.nn.sigmoid(gate_pre) * up_pre).astype(jnp.bfloat16)
    result = jnp.einsum('...b,ba->...a', hidden.astype(jnp.float32), w_two.astype(jnp.float32))
    return result.astype(jnp.bfloat16)

def block_sum(left, right):
    left_blocks = left.reshape(N_TOK, CTOK, left.shape[-1]).astype(jnp.float32)
    right_blocks = right.reshape(N_TOK, CTOK, right.shape[-1]).astype(jnp.float32)
    partials = jnp.einsum('nta,ntb->nab', left_blocks, right_blocks)
    rounded = lax.optimization_barrier(partials.astype(jnp.bfloat16))
    return lax.optimization_barrier(jnp.sum(rounded.astype(jnp.float32), axis=0))

def head_gradient(keys_head, values_head, rates_head, w_one, w_three, w_two):
    gate_pre = jnp.dot(keys_head, w_one, preferred_element_type=jnp.float32)
    up_pre = jnp.dot(keys_head, w_three, preferred_element_type=jnp.float32)
    sigma = jax.nn.sigmoid(gate_pre)
    hidden = (gate_pre * sigma * up_pre).astype(jnp.bfloat16)
    scaled = (-rates_head[:, None] * values_head.astype(jnp.float32)).astype(jnp.bfloat16)
    back = jnp.dot(scaled, w_two.T, preferred_element_type=jnp.float32)
    d_up = (back * gate_pre * sigma).astype(jnp.bfloat16)
    d_gate = (back * up_pre * sigma * (1.0 + gate_pre * (1.0 - sigma))).astype(jnp.bfloat16)
    grad_one = block_sum(keys_head, d_gate)
    grad_three = block_sum(keys_head, d_up)
    grad_two = block_sum(hidden, scaled)
    return (grad_one, grad_three, grad_two)

def renew(weight, grad, rate):
    mean_sq = jnp.mean(grad * grad)
    return (weight.astype(jnp.float32) - rate * grad * lax.rsqrt(mean_sq + 1e-05)).astype(jnp.bfloat16)

def per_head(operands):
    query_head, keys_head, values_head, rates_head, w_one, w_three, w_two, rate = operands
    results = []
    for sequence in range(SEQS):
        first = swiglu_apply(query_head[sequence, 0], w_one, w_three, w_two)
        grad_one, grad_three, grad_two = head_gradient(keys_head[sequence], values_head[sequence], rates_head[sequence], w_one, w_three, w_two)
        new_one = renew(w_one, grad_one, rate)
        new_three = renew(w_three, grad_three, rate)
        new_two = renew(w_two, grad_two, rate)
        second = swiglu_apply(query_head[sequence, 1], new_one, new_three, new_two)
        results.append(jnp.stack([first, second]))
    return jnp.stack(results)

def reference(queries, first_keys, first_values, first_rates, w_one, w_three, w_two, step_size, out_gain):
    query_heads = jnp.moveaxis(queries.reshape(SEQS, GROUPS, GROUP, HEADS, HD), 3, 0)
    key_heads = jnp.moveaxis(first_keys.reshape(SEQS, GROUP, HEADS, HD), 2, 0)
    value_heads = jnp.moveaxis(first_values.reshape(SEQS, GROUP, HEADS, HD), 2, 0)
    rate_heads = jnp.moveaxis(first_rates, 1, 0)
    outputs = lax.map(per_head, (query_heads, key_heads, value_heads, rate_heads, w_one, w_three, w_two, step_size))
    merged = jnp.moveaxis(outputs, 0, 3).reshape(SEQS, GROUPS, GROUP, WIDTH).astype(jnp.float32)
    mean_sq = lax.optimization_barrier(jnp.mean(merged * merged, axis=-1, keepdims=True))
    return (merged * lax.rsqrt(mean_sq + 1e-06) * out_gain).astype(jnp.bfloat16)
```

```python
import functools

import jax
import jax.numpy as jnp
from jax import lax
from jax.experimental import pallas as pl
from jax.experimental.pallas import tpu as pltpu
from jax.sharding import Mesh
from jax.sharding import PartitionSpec as P


BF = jnp.bfloat16
F32 = jnp.float32
TOK = ("zl", "x", "c")
TOK_HEAD = ("zl", "x", "c", "y", "zh")
HD = 512
TOKENS = 256
QUARTER = 384
HALF = 192
SUB = 96


def shape(*dims, dtype=BF):
    return jax.ShapeDtypeStruct(dims, dtype)


def kernel_call(body, outs, args, name, scratch=(), flops=0, aliases=None, out_specs=None):
    vmem = pl.BlockSpec(memory_space=pltpu.VMEM)
    moved = sum(a.size * a.dtype.itemsize for a in list(args) + list(outs))
    return pl.pallas_call(
        body,
        out_shape=list(outs),
        in_specs=[vmem] * len(args),
        out_specs=[vmem] * len(outs),
        scratch_shapes=list(scratch),
        compiler_params=pltpu.CompilerParams(vmem_limit_bytes=32 << 20),
        cost_estimate=pl.CostEstimate(flops=flops, bytes_accessed=moved, transcendentals=0),
        name=name,
    )(*args)


def dot(a, b, dims=((1,), (0,))):
    return lax.dot_general(a, b, (dims, ((), ())), preferred_element_type=F32)


def swiglu(rows, w_one, w_three, w_two):
    gate = dot(rows, w_one)
    up = dot(rows, w_three)
    hidden = (gate * jax.nn.sigmoid(gate) * up).astype(BF)
    return dot(hidden, w_two).astype(BF)


def split_body(keys, values, rates, own_0, own_1, send_0, send_1):
    core = lax.axis_index("c")
    mine = pl.multiple_of(core * HD, HD)
    other = pl.multiple_of((1 - core) * HD, HD)
    for s, own, send in ((0, own_0, send_0), (1, own_1, send_1)):
        columns = jnp.transpose(rates[s])
        mine_rate = jnp.where(core == 0, columns[:, 0:1], columns[:, 1:2])
        other_rate = jnp.where(core == 0, columns[:, 1:2], columns[:, 0:1])
        own[0] = keys[s, :, pl.ds(mine, HD)]
        own[1] = (-mine_rate * values[s, :, pl.ds(mine, HD)].astype(F32)).astype(BF)
        send[0] = keys[s, :, pl.ds(other, HD)]
        send[1] = (-other_rate * values[s, :, pl.ds(other, HD)].astype(F32)).astype(BF)


def queries_body(queries, own, send):
    core = lax.axis_index("c")
    mine = pl.multiple_of(core * HD, HD)
    other = pl.multiple_of((1 - core) * HD, HD)
    for s in range(2):
        own[s] = queries[s, 1, :, pl.ds(mine, HD)]
        send[s] = queries[s, 1, :, pl.ds(other, HD)]


def first_body(queries, w_one, w_three, w_two, out):
    for s in range(2):
        for h in range(2):
            rows = queries[s, 0, :, h * HD : (h + 1) * HD]
            result = swiglu(rows, w_one[h], w_three[h], w_two[h])
            out[:, s, h] = result.reshape(8, 32, HD)


def grads_body(
    own, came, w_one, w_three, w_two, far_a, far_b, right, left, kept, keys, scaled, hid, dg, du, whole
):
    core = lax.axis_index("c")
    place = lax.axis_index("x")
    for part, source in enumerate((own, came)):
        rows = pl.ds(part * TOKENS, TOKENS)
        k, v = source[0], source[1]
        keys[rows] = k
        scaled[rows] = v
        gate = dot(k, w_one[core])
        up = dot(k, w_three[core])
        sig = jax.nn.sigmoid(gate)
        back = dot(v, w_two[core], ((1,), (1,)))
        hid[rows] = (gate * sig * up).astype(BF)
        du[rows] = (back * gate * sig).astype(BF)
        dg[rows] = (back * up * sig * (1.0 + gate * (1.0 - sig))).astype(BF)
    over = ((0,), (0,))
    whole[0:HD] = dot(keys[...], dg[...], over).astype(BF)
    whole[HD : 2 * HD] = dot(keys[...], du[...], over).astype(BF)
    whole[2 * HD : 3 * HD] = dot(hid[...], scaled[...], over).astype(BF)

    def at(step, extra, size):
        start = lax.rem(place + step, 4) * QUARTER + extra
        return whole[pl.ds(pl.multiple_of(start, SUB), size)]

    far_a[...] = at(2, 0, HALF)
    far_b[...] = at(2, HALF, HALF)
    right[...] = at(1, 0, QUARTER)
    left[...] = at(3, 0, QUARTER)
    kept[...] = at(0, 0, QUARTER)


def add(*terms):
    total = terms[0].astype(F32)
    for term in terms[1:]:
        total = total + term.astype(F32)
    return total


def passing_body(right, left, came_a, came_b, right_out, left_out):
    right_out[0:HALF] = add(right[0:HALF], came_a[...]).astype(BF)
    right_out[HALF:QUARTER] = right[HALF:QUARTER]
    left_out[0:HALF] = left[0:HALF]
    left_out[HALF:QUARTER] = add(left[HALF:QUARTER], came_b[...]).astype(BF)


def quarter_body(kept, from_left, from_right, mine, to_1, to_2, to_3):
    level = lax.axis_index("zl")
    for k, out in enumerate((mine, to_1, to_2, to_3)):
        rows = pl.ds(pl.multiple_of((level ^ k) * SUB, SUB), SUB)
        out[...] = add(kept[rows], from_left[rows], from_right[rows]).astype(out.dtype)


def sixteenth_body(mine, came_1, came_2, came_3, out):
    out[...] = add(mine[...], came_1[...], came_2[...], came_3[...]).astype(BF)


def pair_body(upper, lower, out):
    out[0:SUB] = upper[...]
    out[SUB:HALF] = lower[...]


def second_body(
    near, far, near_l, far_l, near_r, far_r, near_x, far_x,
    w_one, w_three, w_two, step, rows_own, rows_came, out, grad, fresh,
):
    core = lax.axis_index("c")
    place = lax.axis_index("x")
    level = lax.axis_index("zl")
    pieces = ((0, near, far), (3, near_l, far_l), (1, near_r, far_r), (2, near_x, far_x))
    for shift, close, distant in pieces:
        base = lax.rem(place + shift, 4) * QUARTER
        for k in range(4):
            start = pl.multiple_of(base + (level ^ k) * SUB, SUB)
            source = close if k < 2 else distant
            at = (k % 2) * SUB
            grad[pl.ds(start, SUB)] = source[at : at + SUB]
    rate = step[core]
    for m, weight in enumerate((w_one, w_three, w_two)):
        g = grad[m * HD : (m + 1) * HD].astype(F32)
        square = jnp.sum(jnp.sum(g * g, axis=0, keepdims=True), axis=1, keepdims=True)
        factor = rate * lax.rsqrt(square * (1.0 / (HD * HD)) + 1e-05)
        fresh[m] = (weight[core].astype(F32) - factor * g).astype(BF)
    for index, rows in ((core, rows_own), (1 - core, rows_came)):
        result = swiglu(rows[...], fresh[0], fresh[1], fresh[2])
        out[:, index] = result.reshape(8, 32, HD)


def second_call(args):
    vmem = pl.BlockSpec(memory_space=pltpu.VMEM)
    smem = pl.BlockSpec(memory_space=pltpu.SMEM)
    specs = [vmem] * len(args)
    specs[11] = smem
    return pl.pallas_call(
        second_body,
        out_shape=shape(8, 2, 32, HD),
        in_specs=specs,
        out_specs=vmem,
        scratch_shapes=[pltpu.VMEM((3 * HD, HD), BF), pltpu.VMEM((3, HD, HD), BF)],
        compiler_params=pltpu.CompilerParams(vmem_limit_bytes=32 << 20),
        cost_estimate=pl.CostEstimate(flops=6 * HD**3, bytes_accessed=8 << 20, transcendentals=0),
        name="second",
    )(*args)


def normalize(blocks, gain_ref):
    total = jnp.zeros((32, HD), F32)
    for i in range(16):
        block = blocks(i).astype(F32)
        total = total + block * block
    scale = lax.rsqrt(jnp.sum(total, axis=1, keepdims=True) * (1.0 / 8192) + 1e-06)
    for i in range(16):
        columns = slice(i * HD, (i + 1) * HD)
        yield columns, (blocks(i).astype(F32) * scale * gain_ref[:, columns]).astype(BF)


def norm_first_body(blocks, gain, out):
    for s in range(2):
        for columns, value in normalize(lambda i: blocks[i // 2, s, i % 2], gain):
            out[s, 0, :, columns] = value


def norm_second_body(blocks, gain, held, out):
    del held
    for columns, value in normalize(lambda i: blocks[i], gain):
        out[0, 0, :, columns] = value


def norm_first(blocks, gain):
    whole = pl.BlockSpec((8, 2, 2, 32, HD), lambda i: (0, 0, 0, 0, 0))
    return pl.pallas_call(
        norm_first_body,
        grid=(1,),
        out_shape=shape(2, 2, 32, 8192),
        in_specs=[whole, pl.BlockSpec((1, 8192), lambda i: (0, 0))],
        out_specs=pl.BlockSpec((2, 1, 32, 8192), lambda i: (0, 0, 0, 0)),
        compiler_params=pltpu.CompilerParams(vmem_limit_bytes=32 << 20),
        cost_estimate=pl.CostEstimate(flops=1 << 20, bytes_accessed=2 << 20, transcendentals=0),
        name="norm_first",
    )(blocks, gain)


def norm_second(blocks, gain, held, s):
    return pl.pallas_call(
        norm_second_body,
        grid=(1,),
        out_shape=shape(2, 2, 32, 8192),
        in_specs=[
            pl.BlockSpec((16, 32, HD), lambda i: (0, 0, 0)),
            pl.BlockSpec((1, 8192), lambda i: (0, 0)),
            pl.BlockSpec(memory_space=pl.ANY),
        ],
        out_specs=pl.BlockSpec((1, 1, 32, 8192), lambda i: (s, 1, 0, 0)),
        input_output_aliases={2: 0},
        compiler_params=pltpu.CompilerParams(vmem_limit_bytes=32 << 20),
        cost_estimate=pl.CostEstimate(flops=1 << 19, bytes_accessed=1 << 20, transcendentals=0),
        name="norm_second",
    )(blocks, gain, held)


def shift(array, axis, by):
    size = lax.axis_size(axis)
    return lax.ppermute(array, axis, [(i, (i + by) % size) for i in range(size)])


def flip(array, axis, by):
    return lax.ppermute(array, axis, [(i, i ^ by) for i in range(lax.axis_size(axis))])


def reduced(own, came, weights):
    far_a, far_b, right, left, kept = kernel_call(
        grads_body,
        [shape(HALF, HD)] * 2 + [shape(QUARTER, HD)] * 3,
        (own, came, *weights),
        "grads",
        [pltpu.VMEM((2 * TOKENS, HD), BF)] * 5 + [pltpu.VMEM((3 * HD, HD), BF)],
        flops=12 * HD**3,
    )
    came_a, came_b = shift(far_a, "x", 1), shift(far_b, "x", -1)
    right, left = kernel_call(
        passing_body, [shape(QUARTER, HD)] * 2, (right, left, came_a, came_b), "passing"
    )
    from_left, from_right = shift(right, "x", 1), shift(left, "x", -1)
    mine, to_1, to_2, to_3 = kernel_call(
        quarter_body,
        [shape(SUB, HD, dtype=F32)] + [shape(SUB, HD)] * 3,
        (kept, from_left, from_right),
        "quarter",
    )
    arrived = [flip(a, "zl", k) for k, a in ((1, to_1), (2, to_2), (3, to_3))]
    (summed,) = kernel_call(sixteenth_body, [shape(SUB, HD)], (mine, *arrived), "sixteenth")
    return summed


def gathered(summed):
    arrived = [flip(summed, "zl", k) for k in (1, 2, 3)]
    (near,) = kernel_call(pair_body, [shape(HALF, HD)], (summed, arrived[0]), "pair")
    (far,) = kernel_call(pair_body, [shape(HALF, HD)], (arrived[1], arrived[2]), "pair")
    near_l, near_r = shift(near, "x", 1), shift(near, "x", -1)
    far_r, far_l = shift(far, "x", -1), shift(far, "x", 1)
    near_x, far_x = shift(near_l, "x", 1), shift(far_r, "x", -1)
    return near, far, near_l, far_l, near_r, far_r, near_x, far_x


def shards(
    queries, first_keys, first_values, first_rates, w_one, w_three, w_two, step_size, out_gain
):
    weights = (w_one, w_three, w_two)
    gain = out_gain.reshape(1, 8192)
    own_0, own_1, send_0, send_1 = kernel_call(
        split_body,
        [shape(2, TOKENS, HD)] * 4,
        (first_keys, first_values, first_rates),
        "split",
    )
    summed = []
    for own, send in ((own_0, send_0), (own_1, send_1)):
        summed.append(reduced(own, flip(send, "c", 1), weights))
    rows_own, rows_send = kernel_call(
        queries_body, [shape(2, TOKENS, HD)] * 2, (queries,), "queries"
    )
    rows_came = flip(rows_send, "c", 1)
    (first,) = kernel_call(
        first_body, [shape(8, 2, 2, 32, HD)], (queries, *weights), "first", flops=24 * HD**3
    )
    first = lax.all_to_all(first, ("y", "zh"), 0, 0, tiled=True)
    out = norm_first(first, gain)
    for s in range(2):
        result = second_call(
            (*gathered(summed[s]), *weights, step_size, rows_own[s], rows_came[s])
        )
        moved = lax.all_to_all(
            result.reshape(16, 32, HD), ("y", "zh", "c"), 0, 0, tiled=True
        )
        out = norm_second(moved, gain, out, s)
    return out


def solution(mesh):
    finer = Mesh(mesh.devices.reshape(4, 4, 2, 4, 2), TOK_HEAD)
    heads = ("y", "zh")
    in_specs = (
        P(None, None, TOK, heads),
        P(None, TOK, heads),
        P(None, TOK, heads),
        P(None, heads, TOK),
        P(heads, None, None),
        P(heads, None, None),
        P(heads, None, None),
        P(heads),
        P(),
    )
    out_specs = P(None, None, TOK_HEAD, None)
    return jax.shard_map(
        shards, mesh=finer, in_specs=in_specs, out_specs=out_specs, check_vma=False
    )
```

```python
import functools

import jax
import jax.numpy as jnp
from jax import lax
from jax.experimental import pallas as pl
from jax.experimental.pallas import tpu as pltpu
from jax.sharding import Mesh
from jax.sharding import PartitionSpec as P


BF = jnp.bfloat16
F32 = jnp.float32
TOK = ("zl", "x", "c")
TOK_HEAD = ("zl", "x", "c", "y", "zh")
HD = 512
TOKENS = 256
QUARTER = 384
HALF = 192
SUB = 96


def shape(*dims, dtype=BF):
    return jax.ShapeDtypeStruct(dims, dtype)


def kernel_call(body, outs, args, scratch=(), flops=0, spaces=None, out_space=None, aliases=None):
    spaces = spaces or {}
    specs = [pl.BlockSpec(memory_space=spaces.get(i, pltpu.VMEM)) for i in range(len(args))]
    args = [
        pltpu.with_memory_space_constraint(a, pltpu.HBM) if i in spaces and spaces[i] == pltpu.HBM else a
        for i, a in enumerate(args)
    ]
    moved = sum(a.size * a.dtype.itemsize for a in list(args) + list(outs))
    return pl.pallas_call(
        body,
        out_shape=list(outs),
        in_specs=specs,
        out_specs=[pl.BlockSpec(memory_space=out_space or pltpu.VMEM)] * len(outs),
        scratch_shapes=list(scratch),
        input_output_aliases=aliases or {},
        compiler_params=pltpu.CompilerParams(vmem_limit_bytes=24 << 20),
        cost_estimate=pl.CostEstimate(flops=flops, bytes_accessed=moved, transcendentals=0),
    )(*args)


def far_away(*indices):
    return {i: pltpu.HBM for i in indices}


def dot(a, b, dims=((1,), (0,))):
    return lax.dot_general(a, b, (dims, ((), ())), preferred_element_type=F32)


def swiglu(rows, w_one, w_three, w_two):
    gate = dot(rows, w_one)
    up = dot(rows, w_three)
    hidden = (gate * jax.nn.sigmoid(gate) * up).astype(BF)
    return dot(hidden, w_two).astype(BF)


def copies(pairs, sems):
    made = [pltpu.make_async_copy(src, dst, sems.at[i]) for i, (src, dst) in enumerate(pairs)]
    for copy in made:
        copy.start()
    return made


def columns_of(head):
    return pl.ds(pl.multiple_of(head * HD, HD), HD)


def scaled_rows(rates, head, rows):
    columns = jnp.transpose(rates[...])
    rate = jnp.where(head == 0, columns[:, 0:1], columns[:, 1:2])
    return (-rate * rows.astype(F32)).astype(BF)


def send_body(
    keys, values, rates, queries, own_0, own_1, send_0, send_1, rows, raw, rate, sems
):
    core = lax.axis_index("c")
    heads = (core, 1 - core)
    outs = ((own_0, send_0), (own_1, send_1))
    pairs = [(rates, rate)]
    for s in range(2):
        for i in (1, 0):
            pairs.append((values.at[s, :, columns_of(heads[i])], raw.at[s, i]))
            pairs.append((keys.at[s, :, columns_of(heads[i])], outs[s][i].at[0]))
    for s in range(2):
        pairs.append((queries.at[s, 1, :, columns_of(1 - core)], rows.at[s]))
    made = copies(pairs, sems)
    made[0].wait()
    at = 1
    for s in range(2):
        for i in (1, 0):
            made[at].wait()
            outs[s][i][1] = scaled_rows(rate.at[s], heads[i], raw[s, i])
            made[at + 1].wait()
            at += 2
    for copy in made[at:]:
        copy.wait()


def first_body(
    queries, w_one, w_three, w_two, out_0, out_1, out_2, out_3, rows, one, three, two, result, sems
):
    made = copies(
        [(queries.at[s, 0], rows.at[s]) for s in range(2)]
        + [
            (matrix.at[h], held.at[h])
            for h in range(2)
            for matrix, held in ((w_one, one), (w_three, three), (w_two, two))
        ],
        sems,
    )
    made[0].wait()
    made[1].wait()
    y, zh = lax.axis_index("y"), lax.axis_index("zh")
    for h in range(2):
        for copy in made[2 + 3 * h : 5 + 3 * h]:
            copy.wait()
        for s in range(2):
            values = swiglu(rows[s, :, h * HD : (h + 1) * HD], one[h], three[h], two[h])
            result[...] = values.reshape(8, 32, HD)
            for k, out in enumerate((out_0, out_1, out_2, out_3)):
                for z in range(2):
                    out[z, s, h] = result[lax.rem(y + k, 4) * 2 + (zh ^ z)]


def across_body(*refs):
    for k in range(4):
        refs[4][k] = refs[k][1]


def put_rows(rows, weights, result, out, sems):
    core = lax.axis_index("c")
    back = []
    for i, (index, source) in enumerate(((core, rows[0]), (1 - core, rows[1]))):
        result[i] = swiglu(source[...], weights[0], weights[1], weights[2]).reshape(8, 32, HD)
        copy = pltpu.make_async_copy(result.at[i], out.at[:, index], sems.at[i])
        copy.start()
        back.append(copy)
    for copy in back:
        copy.wait()


def grads_body(
    own, came, w_one, w_three, w_two, far_a, far_b, right, left, kept,
    keys, scaled, hid, dg, du, whole,
):
    core = lax.axis_index("c")
    place = lax.axis_index("x")
    one, three, two = w_one.at[core], w_three.at[core], w_two.at[core]
    for part, source in enumerate((own, came)):
        rows = pl.ds(part * TOKENS, TOKENS)
        keys[rows] = source[0]
        scaled[rows] = source[1]
    for part in range(2):
        rows = pl.ds(part * TOKENS, TOKENS)
        gate = dot(keys[rows], one[...])
        up = dot(keys[rows], three[...])
        sig = jax.nn.sigmoid(gate)
        back = dot(scaled[rows], two[...], ((1,), (1,)))
        hid[rows] = (gate * sig * up).astype(BF)
        du[rows] = (back * gate * sig).astype(BF)
        dg[rows] = (back * up * sig * (1.0 + gate * (1.0 - sig))).astype(BF)
    over = ((0,), (0,))
    whole[0:HD] = dot(keys[...], dg[...], over).astype(BF)
    whole[HD : 2 * HD] = dot(keys[...], du[...], over).astype(BF)
    whole[2 * HD : 3 * HD] = dot(hid[...], scaled[...], over).astype(BF)

    def at(step, extra, size):
        start = lax.rem(place + step, 4) * QUARTER + extra
        return whole[pl.ds(pl.multiple_of(start, SUB), size)]

    far_a[...] = at(2, 0, HALF)
    far_b[...] = at(2, HALF, HALF)
    right[...] = at(1, 0, QUARTER)
    left[...] = at(3, 0, QUARTER)
    kept[...] = at(0, 0, QUARTER)


def add(*terms):
    total = terms[0].astype(F32)
    for term in terms[1:]:
        total = total + term.astype(F32)
    return total


def passing_body(right, left, came_a, came_b, right_out, left_out):
    right_out[0:HALF] = add(right[0:HALF], came_a[...]).astype(BF)
    right_out[HALF:QUARTER] = right[HALF:QUARTER]
    left_out[0:HALF] = left[0:HALF]
    left_out[HALF:QUARTER] = add(left[HALF:QUARTER], came_b[...]).astype(BF)


def quarter_body(kept, from_left, from_right, mine, send):
    level = lax.axis_index("zl")
    for k, (out, at) in enumerate(((mine, 0), (send, 0), (mine, SUB), (send, SUB))):
        rows = pl.ds(pl.multiple_of((level ^ k) * SUB, SUB), SUB)
        total = add(kept[rows], from_left[rows], from_right[rows])
        out[at : at + SUB] = total.astype(out.dtype)


def middle_body(mine, came, kept, send):
    kept[...] = add(mine[0:SUB], came[0:SUB])
    send[...] = add(mine[SUB:HALF], came[SUB:HALF]).astype(BF)


def sixteenth_body(mine, came, out):
    out[...] = add(mine[...], came[...]).astype(BF)


def join_body(upper, lower, out):
    rows = upper.shape[0]
    out[0:rows] = upper[...]
    out[rows : 2 * rows] = lower[...]


PLACES = (0, 2, 1, 3)


def second_body(s, pieces, *refs):
    inputs = pieces[-1][1][-1] + 1
    w_one, w_three, w_two, step, queries, rows_came = refs[inputs : inputs + 6]
    out, grad, fresh, one, rows, result, back_sem, sems = refs[-8:]
    core = lax.axis_index("c")
    place = lax.axis_index("x")
    level = lax.axis_index("zl")
    made = copies(
        (
            (w_one.at[core], one.at[0]),
            (w_three.at[core], one.at[1]),
            (w_two.at[core], one.at[2]),
            (queries.at[s, 1, :, columns_of(core)], rows),
        ),
        sems,
    )
    for distance, indices in pieces:
        base = lax.rem(place + distance, 4) * QUARTER
        each = 4 // len(indices)
        for k in range(4):
            start = pl.multiple_of(base + (level ^ PLACES[k]) * SUB, SUB)
            source = refs[indices[k // each]]
            grad[pl.ds(start, SUB)] = source[pl.ds((k % each) * SUB, SUB)]
    rate = step[core]
    factors = []
    for m in range(3):
        g = grad[m * HD : (m + 1) * HD].astype(F32)
        square = jnp.sum(jnp.sum(g * g, axis=0, keepdims=True), axis=1, keepdims=True)
        factors.append(rate * lax.rsqrt(square * (1.0 / (HD * HD)) + 1e-05))
    for m in range(3):
        made[m].wait()
        g = grad[m * HD : (m + 1) * HD].astype(F32)
        fresh[m] = (one[m].astype(F32) - factors[m] * g).astype(BF)
    made[3].wait()
    put_rows((rows, rows_came.at[s]), fresh, result, out, back_sem)


def normalize(blocks, gain_ref):
    total = jnp.zeros((32, HD), F32)
    for i in range(16):
        block = blocks(i).astype(F32)
        total = total + block * block
    scale = lax.rsqrt(jnp.sum(total, axis=1, keepdims=True) * (1.0 / 8192) + 1e-06)
    for i in range(16):
        columns = slice(i * HD, (i + 1) * HD)
        yield columns, (blocks(i).astype(F32) * scale * gain_ref[:, columns]).astype(BF)


def norm_body(blocks, gain, *refs):
    for columns, value in normalize(lambda i: blocks[i], gain):
        refs[-1][0, 0, :, columns] = value


def norm_first_body(near_0, near_1, near_2, near_3, far, gain, out):
    y, zh = lax.axis_index("y"), lax.axis_index("zh")
    for s in range(2):
        pieces = []
        for k, near in enumerate((near_0, near_1, near_2, near_3)):
            for z in range(2):
                for h in range(2):
                    head = (lax.rem(y + 4 - k, 4) * 2 + (zh ^ z)) * 2 + h
                    pieces.append((columns_of(head), near.at[0, s, h] if z == 0 else far.at[k, s, h]))
        total = jnp.zeros((32, HD), F32)
        for _, piece in pieces:
            block = piece[...].astype(F32)
            total = total + block * block
        scale = lax.rsqrt(jnp.sum(total, axis=1, keepdims=True) * (1.0 / 8192) + 1e-06)
        for columns, piece in pieces:
            out[s, 0, :, columns] = (piece[...].astype(F32) * scale * gain[:, columns]).astype(BF)


def norm(blocks, gain, held, s):
    row = pl.BlockSpec((1, 8192), lambda i: (0, 0))
    if held is None:
        body, args = norm_first_body, (*blocks, gain)
        specs = [pl.BlockSpec(a.shape, lambda i: (0, 0, 0, 0, 0)) for a in blocks] + [row]
        out_spec = pl.BlockSpec((2, 1, 32, 8192), lambda i: (0, 0, 0, 0))
    else:
        body, args = norm_body, (blocks, gain, held)
        specs = [pl.BlockSpec((16, 32, HD), lambda i: (0, 0, 0)), row]
        specs.append(pl.BlockSpec(memory_space=pl.ANY))
        out_spec = pl.BlockSpec((1, 1, 32, 8192), lambda i: (s, 1, 0, 0))
    return pl.pallas_call(
        body,
        grid=(1,),
        out_shape=shape(2, 2, 32, 8192),
        in_specs=specs,
        out_specs=out_spec,
        input_output_aliases={} if held is None else {2: 0},
        compiler_params=pltpu.CompilerParams(vmem_limit_bytes=24 << 20),
        cost_estimate=pl.CostEstimate(flops=1 << 19, bytes_accessed=1 << 20, transcendentals=0),
    )(*args)


def shift(array, axis, by):
    size = lax.axis_size(axis)
    return lax.ppermute(array, axis, [(i, (i + by) % size) for i in range(size)])


def flip(array, axis, by):
    return lax.ppermute(array, axis, [(i, i ^ by) for i in range(lax.axis_size(axis))])


def exchange(array, axes):
    return lax.all_to_all(array, axes, 0, 0, tiled=True)


def block(*dims):
    return pltpu.VMEM(dims, BF)


def sems(count):
    return pltpu.SemaphoreType.DMA((count,))


def shards(
    queries, first_keys, first_values, first_rates, w_one, w_three, w_two, step_size, out_gain
):
    return layer(
        queries, first_keys, first_values, first_rates, (w_one, w_three, w_two), step_size, out_gain
    )


def layer(queries, keys, values, rates, weights, step_size, out_gain):
    gain = out_gain.reshape(1, 8192)
    pending, kept = [], []
    own_0, own_1, send_0, send_1, rows_send = kernel_call(
        send_body,
        [shape(2, TOKENS, HD)] * 5,
        (keys, values, rates, queries),
        [block(2, 2, TOKENS, HD), pltpu.VMEM((2, 2, TOKENS), F32), sems(11)],
        spaces=far_away(0, 1, 2, 3),
    )
    swapped = [flip(send_0, "c", 1), flip(send_1, "c", 1)]
    for s, own in enumerate((own_0, own_1)):
        far_a, far_b, right, left, own = kernel_call(
            grads_body,
            [shape(HALF, HD)] * 2 + [shape(QUARTER, HD)] * 3,
            (own, swapped[s], *weights),
            [block(2 * TOKENS, HD)] * 5 + [block(3 * HD, HD)],
            flops=12 * HD**3,
        )
        came_a, came_b = shift(far_a, "x", 1), shift(far_b, "x", -1)
        right, left = kernel_call(
            passing_body, [shape(QUARTER, HD)] * 2, (right, left, came_a, came_b)
        )
        pending.append((shift(right, "x", 1), shift(left, "x", -1)))
        kept.append(own)
    firsts = kernel_call(
        first_body,
        [shape(2, 2, 2, 32, HD)] * 4,
        (queries, *weights),
        [block(2, TOKENS, 2 * HD)] + [block(2, HD, HD)] * 3 + [block(8, 32, HD), sems(8)],
        flops=24 * HD**3,
        spaces=far_away(0),
    )
    nears = [firsts[0]] + [shift(firsts[k], "y", k) for k in (1, 2, 3)]
    rows_came = flip(rows_send, "c", 1)
    (over,) = kernel_call(across_body, [shape(4, 2, 2, 32, HD)], nears)
    fars = flip(over, "zh", 1)
    halves = []
    for s in range(2):
        mine, send = kernel_call(
            quarter_body, [shape(HALF, HD, dtype=F32), shape(HALF, HD)], (kept[s], *pending[s])
        )
        mine, send = kernel_call(
            middle_body, [shape(SUB, HD, dtype=F32), shape(SUB, HD)], (mine, flip(send, "zl", 1))
        )
        (summed,) = kernel_call(sixteenth_body, [shape(SUB, HD)], (mine, flip(send, "zl", 2)))
        (near,) = kernel_call(join_body, [shape(HALF, HD)], (summed, flip(summed, "zl", 2)))
        halves.append((near, flip(near, "zl", 1)))

    def second(s, parts, layout):
        count = len(parts)
        (result,) = kernel_call(
            functools.partial(second_body, s, layout),
            [shape(8, 2, 32, HD)],
            (*parts, *weights, step_size, queries, rows_came),
            [block(3 * HD, HD), block(3, HD, HD), block(3, HD, HD), block(TOKENS, HD)]
            + [block(2, 8, 32, HD), sems(2), sems(4)],
            flops=6 * HD**3,
            spaces={
                **far_away(*(count + i for i in (0, 1, 2, 4))),
                count + 3: pltpu.SMEM,
            },
            out_space=pltpu.HBM,
        )
        return exchange(result.reshape(16, 32, HD), ("y", "zh", "c"))

    (quad,) = kernel_call(join_body, [shape(QUARTER, HD)], halves[0])
    parts = (quad, shift(quad, "x", 1), shift(quad, "x", -1), shift(quad, "x", 2))
    arrived_0 = second(0, parts, ((0, (0,)), (3, (1,)), (1, (2,)), (2, (3,))))

    near, far = halves[1]
    near_l, far_r = shift(near, "x", 1), shift(far, "x", -1)
    near_r, far_l = shift(near, "x", -1), shift(far, "x", 1)
    near_x, far_x = shift(near_l, "x", 1), shift(far_r, "x", -1)
    parts = (near, far, near_l, far_l, near_r, far_r, near_x, far_x)
    arrived_1 = second(1, parts, ((0, (0, 1)), (3, (2, 3)), (1, (4, 5)), (2, (6, 7))))
    out = norm((*nears, fars), gain, None, 0)
    out = norm(arrived_0, gain, out, 0)
    return norm(arrived_1, gain, out, 1)


def solution(mesh):
    finer = Mesh(mesh.devices.reshape(4, 4, 2, 4, 2), TOK_HEAD)
    heads = ("y", "zh")
    in_specs = (
        P(None, None, TOK, heads),
        P(None, TOK, heads),
        P(None, TOK, heads),
        P(None, heads, TOK),
        P(heads, None, None),
        P(heads, None, None),
        P(heads, None, None),
        P(heads),
        P(),
    )
    out_specs = P(None, None, TOK_HEAD, None)
    return jax.shard_map(
        shards, mesh=finer, in_specs=in_specs, out_specs=out_specs, check_vma=False
    )
```
